32 devices in a mesh: row: 8 (over z, x), col: 4 (over y, core).
Axes of the slice: x: 2, y: 2, z: 4, core: 2. Of those that a mesh axis runs over, the one named last changes fastest.
Arguments:
- panel_block: float32 [24576, 512], P('row', 'col'), may hold values from -1 to 1
- trailing: float32 [24576, 2048], P('row', 'col'), may hold values from -6 to 6
Outputs:
- triangle: float32 [512, 512], replicated
- coupling: float32 [512, 2048], P(None, 'col')
- updated: float32 [24576, 2048], P('row', 'col')
The draws below stay inside these ranges and needn't reach their ends.
All inputs are finite; a program needn't handle non-finite values.
Results may differ from the reference program's by a relative error of at most 0.0003.
Values sent between devices are 32-bit elements; how exact they have to be, the bound alone decides.
A program may use at most 128 MiB of HBM per device.

```python
import jax
import jax.numpy as jnp
from jax import lax

B = 512
NC = 2048
ROWS = 24576


def draw_panel_block(key, part):
    first_key, second_key = jax.random.split(key)
    base = jax.random.normal(first_key, (ROWS, B), jnp.float32)
    mixing = jnp.eye(B, dtype=jnp.float32) + 0.6 * jax.random.normal(second_key, (B, B), jnp.float32) / B ** 0.5
    return jnp.dot(base, mixing, precision=lax.Precision.HIGHEST) * ROWS ** (-0.5)


def block_scale(rng, dims, pieces, low, top_value):
    gain = 1.0
    for position, shards_of in pieces:
        steps = jax.random.uniform(jax.random.fold_in(jax.random.fold_in(rng, 6), position), (shards_of,), jnp.float32, low / len(pieces), top_value / len(pieces))
        gain = gain * jnp.repeat(jnp.exp(steps), dims[position] // shards_of).reshape((-1,) + (1,) * (len(dims) - 1 - position))
    return gain


def bell_draw(own_key, dims, scale, reach, cuts=(), kind=jnp.bfloat16):
    factor_of = block_scale(own_key, dims, cuts, -0.22, 0.18) if cuts else 1.0
    result = jax.random.normal(own_key, dims, jnp.float32) * scale * factor_of
    return jnp.minimum(jnp.maximum(result, -reach), reach).astype(kind)


def setup_inputs(seed: int = 0) -> dict:
    seeds = jax.random.split(jax.random.key(seed), 3)
    return {
        "panel_block": draw_panel_block(jax.random.fold_in(seeds[2], 71), 0),
        "trailing": bell_draw(seeds[1], (ROWS, NC), 1.0, 6.0, ((0, 8), (1, 4)), jnp.float32),
    }


def reference(panel_block, trailing):
    orthonormal, triangle = jnp.linalg.qr(panel_block)
    sign_fix = jnp.where(jnp.diagonal(triangle) < 0, -1.0, 1.0).astype(jnp.float32)
    triangle = triangle * sign_fix[:, None]
    orthonormal = orthonormal * sign_fix[None, :]
    coupling = jnp.dot(orthonormal.T.astype(jnp.float32), trailing.astype(jnp.float32), precision=lax.Precision.HIGHEST, preferred_element_type=jnp.float32)
    updated = trailing - jnp.dot(orthonormal.astype(jnp.float32), coupling.astype(jnp.float32), precision=lax.Precision.HIGHEST, preferred_element_type=jnp.float32)
    return (triangle, coupling, updated)
```

```python
import jax
import jax.numpy as jnp
from jax import lax
from jax.experimental import pallas as pl
from jax.experimental.pallas import tpu as pltpu
from jax.sharding import PartitionSpec as P

LANES = 128
SUB = 8
highest = lax.Precision.HIGHEST
high = lax.Precision.HIGH


def inner_products(left, right, precision=high):
    return lax.dot_general(
        left, right, (((0,), (0,)), ((), ())), precision=precision, preferred_element_type=jnp.float32
    )


def matmul(left, right, precision=high):
    return jnp.dot(left, right, precision=precision, preferred_element_type=jnp.float32)


def split3(x):
    top = x.astype(jnp.bfloat16).astype(jnp.float32)
    rest = x - top
    mid = rest.astype(jnp.bfloat16).astype(jnp.float32)
    return top, mid, rest - mid


def rank_update(left, right):
    lt, lm, ll = split3(left)
    rt, rm, rl = split3(right)
    a = jnp.concatenate([lt, lt, lm, lt, ll, lm], axis=0).astype(jnp.bfloat16)
    b = jnp.concatenate([rt, rm, rt, rl, rt, rm], axis=0).astype(jnp.bfloat16)
    return lax.dot_general(a, b, (((0,), (0,)), ((), ())), preferred_element_type=jnp.float32)


def factor_diagonal(square):
    lane = lax.broadcasted_iota(jnp.int32, (SUB, LANES), 1)
    sub = lax.broadcasted_iota(jnp.int32, (SUB, LANES), 0)
    full = (SUB, LANES)
    work = square
    upper_rows, inverse_rows = [], []
    for first in range(0, LANES, SUB):
        rows = work[:SUB]
        b = [jnp.broadcast_to(rows[t : t + 1, :], full) for t in range(SUB)]
        d = [
            [None if s < t else jnp.broadcast_to(b[t][:, first + s : first + s + 1], full) for s in range(SUB)]
            for t in range(SUB)
        ]
        inside = (lane >= first) & (lane < first + SUB)
        unit = [jnp.where(inside, jnp.where(lane == first + t, 1.0, 0.0), b[t]) for t in range(SUB)]
        tri = jnp.zeros(full, jnp.float32)
        out = jnp.zeros(full, jnp.float32)
        for t in range(SUB):
            inv = 1.0 / jnp.sqrt(d[t][t])
            for s in range(t, SUB):
                d[t][s] = d[t][s] * inv
            x = unit[t] * inv
            for s in range(t + 1, SUB):
                for q in range(s, SUB):
                    d[s][q] = d[s][q] - d[t][s] * d[t][q]
                unit[s] = unit[s] - d[t][s] * x
            line = x
            for s in range(SUB):
                line = jnp.where(lane == first + s, d[t][s] if s >= t else 0.0, line)
            tri = jnp.where(sub == t, line, tri)
            out = jnp.where(sub == t, x, out)
        upper_rows.append(jnp.where(lane >= first, tri, 0.0))
        inverse_rows.append(jnp.where(lane < first + SUB, out, 0.0))
        if first + SUB < LANES:
            beyond = jnp.where(lane >= first + SUB, out, 0.0)
            left = work[SUB:]
            place = lax.broadcasted_iota(jnp.int32, left.shape, 1)
            left = jnp.where((place >= first) & (place < first + SUB), 0.0, left)
            work = left - rank_update(beyond, out)[first + SUB :]
    return jnp.concatenate(upper_rows, axis=0), jnp.concatenate(inverse_rows, axis=0)


def factor_kernel(gram_ref, upper_ref, inverse_ref, work):
    width = gram_ref.shape[0]
    work[...] = gram_ref[...]
    upper_ref[...] = jnp.zeros_like(upper_ref)
    inverse_ref[...] = jnp.zeros_like(inverse_ref)
    lanes_all = lax.broadcasted_iota(jnp.int32, (LANES, width), 1)

    @pl.loop(0, width // LANES)
    def _(k):
        at = pl.multiple_of(k * LANES, LANES)
        here = pl.ds(at, LANES)
        upper, inverse = factor_diagonal(work[here, here])
        rows = matmul(inverse, work[here, :], highest)
        upper_ref[here, :] = jnp.where(lanes_all >= at + LANES, rows, 0.0)
        upper_ref[here, here] = upper
        inverse_ref[here, :] = jnp.where(lanes_all < at, rows, 0.0)
        inverse_ref[here, here] = inverse
        work[here, :] = rows
        work[here, here] = inverse
        done = work[here, :]
        right = upper_ref[here, :]
        for i in range(1, width // LANES):
            @pl.when(i > k)
            def _():
                block = slice(i * LANES, (i + 1) * LANES)
                below = inner_products(right[:, block], done, highest)
                old = jnp.where((lanes_all >= at) & (lanes_all < at + LANES), 0.0, work[block, :])
                work[block, :] = old - below


def factor(gram):
    width = gram.shape[0]
    spec = pl.BlockSpec(memory_space=pltpu.VMEM)
    shape = jax.ShapeDtypeStruct((width, width), jnp.float32)
    return pl.pallas_call(
        factor_kernel,
        out_shape=(shape, shape),
        in_specs=[spec],
        out_specs=(spec, spec),
        scratch_shapes=[pltpu.VMEM((width, width), jnp.float32)],
        cost_estimate=pl.CostEstimate(
            flops=4 * width**3, bytes_accessed=12 * width * width, transcendentals=100000
        ),
        name="factor",
    )(gram)


def on_device(panel_block, trailing):
    gathered = lax.all_gather(panel_block, "col", axis=1, tiled=True)
    gram_part = lax.psum(inner_products(gathered, panel_block), "row")
    gram = lax.all_gather(gram_part, "col", axis=1, tiled=True)
    share = inner_products(gathered, trailing)
    gram, share = lax.optimization_barrier((gram, share))
    projected = lax.psum(share, "row")
    upper, inverse = factor(gram)
    coupling = matmul(inverse, projected)
    weights = inner_products(inverse, coupling)
    updated = trailing - matmul(gathered, weights)
    return (upper, coupling, updated)


def solution(mesh):
    placed = (P("row", "col"), P("row", "col"))
    return jax.shard_map(
        on_device,
        mesh=mesh,
        in_specs=placed,
        out_specs=(P(), P(None, "col"), P("row", "col")),
        check_vma=False,
    )
```

```python
import functools

import jax
import jax.numpy as jnp
from jax import lax
from jax.experimental import pallas as pl
from jax.experimental.pallas import tpu as pltpu
from jax.sharding import PartitionSpec as P

LANES = 128
SUB = 8
highest = lax.Precision.HIGHEST
high = lax.Precision.HIGH


def inner_products(left, right, precision=high):
    return lax.dot_general(
        left, right, (((0,), (0,)), ((), ())), precision=precision, preferred_element_type=jnp.float32
    )


def matmul(left, right, precision=high):
    return jnp.dot(left, right, precision=precision, preferred_element_type=jnp.float32)


def split3(x):
    top = x.astype(jnp.bfloat16).astype(jnp.float32)
    rest = x - top
    mid = rest.astype(jnp.bfloat16).astype(jnp.float32)
    return top, mid, rest - mid


def rank_update(left, right):
    lt, lm, ll = split3(left)
    rt, rm, rl = split3(right)
    a = jnp.concatenate([lt, lt, lm, lt, ll, lm], axis=0).astype(jnp.bfloat16)
    b = jnp.concatenate([rt, rm, rt, rl, rt, rm], axis=0).astype(jnp.bfloat16)
    return lax.dot_general(a, b, (((0,), (0,)), ((), ())), preferred_element_type=jnp.float32)


def factor_diagonal(square):
    lane = lax.broadcasted_iota(jnp.int32, (SUB, LANES), 1)
    sub = lax.broadcasted_iota(jnp.int32, (SUB, LANES), 0)
    full = (SUB, LANES)
    work = square
    upper_rows, inverse_rows = [], []
    for first in range(0, LANES, SUB):
        rows = work[:SUB]
        b = [jnp.broadcast_to(rows[t : t + 1, :], full) for t in range(SUB)]
        d = [
            [None if s < t else jnp.broadcast_to(b[t][:, first + s : first + s + 1], full) for s in range(SUB)]
            for t in range(SUB)
        ]
        inside = (lane >= first) & (lane < first + SUB)
        unit = [jnp.where(inside, jnp.where(lane == first + t, 1.0, 0.0), b[t]) for t in range(SUB)]
        tri = jnp.zeros(full, jnp.float32)
        out = jnp.zeros(full, jnp.float32)
        for t in range(SUB):
            inv = 1.0 / jnp.sqrt(d[t][t])
            for s in range(t, SUB):
                d[t][s] = d[t][s] * inv
            x = unit[t] * inv
            for s in range(t + 1, SUB):
                for q in range(s, SUB):
                    d[s][q] = d[s][q] - d[t][s] * d[t][q]
                unit[s] = unit[s] - d[t][s] * x
            line = x
            for s in range(SUB):
                line = jnp.where(lane == first + s, d[t][s] if s >= t else 0.0, line)
            tri = jnp.where(sub == t, line, tri)
            out = jnp.where(sub == t, x, out)
        upper_rows.append(jnp.where(lane >= first, tri, 0.0))
        inverse_rows.append(jnp.where(lane < first + SUB, out, 0.0))
        if first + SUB < LANES:
            beyond = jnp.where(lane >= first + SUB, out, 0.0)
            left = work[SUB:]
            place = lax.broadcasted_iota(jnp.int32, left.shape, 1)
            left = jnp.where((place >= first) & (place < first + SUB), 0.0, left)
            work = left - rank_update(beyond, out)[first + SUB :]
    return jnp.concatenate(upper_rows, axis=0), jnp.concatenate(inverse_rows, axis=0)


def factor_kernel(gram_ref, upper_ref, inverse_ref, work):
    width = gram_ref.shape[0]
    work[...] = gram_ref[...]
    upper_ref[...] = jnp.zeros_like(upper_ref)
    inverse_ref[...] = jnp.zeros_like(inverse_ref)
    lanes_all = lax.broadcasted_iota(jnp.int32, (LANES, width), 1)

    @pl.loop(0, width // LANES)
    def _(k):
        at = pl.multiple_of(k * LANES, LANES)
        here = pl.ds(at, LANES)
        upper, inverse = factor_diagonal(work[here, here])
        rows = matmul(inverse, work[here, :], highest)
        upper_ref[here, :] = jnp.where(lanes_all >= at + LANES, rows, 0.0)
        upper_ref[here, here] = upper
        inverse_ref[here, :] = jnp.where(lanes_all < at, rows, 0.0)
        inverse_ref[here, here] = inverse
        work[here, :] = rows
        work[here, here] = inverse
        done = work[here, :]
        right = upper_ref[here, :]
        for i in range(1, width // LANES):
            @pl.when(i > k)
            def _():
                block = slice(i * LANES, (i + 1) * LANES)
                below = inner_products(right[:, block], done, highest)
                old = jnp.where((lanes_all >= at) & (lanes_all < at + LANES), 0.0, work[block, :])
                work[block, :] = old - below


def factor(gram):
    width = gram.shape[0]
    spec = pl.BlockSpec(memory_space=pltpu.VMEM)
    shape = jax.ShapeDtypeStruct((width, width), jnp.float32)
    return pl.pallas_call(
        factor_kernel,
        out_shape=(shape, shape),
        in_specs=[spec],
        out_specs=(spec, spec),
        scratch_shapes=[pltpu.VMEM((width, width), jnp.float32)],
        cost_estimate=pl.CostEstimate(
            flops=4 * width**3, bytes_accessed=12 * width * width, transcendentals=100000
        ),
        name="factor",
    )(gram)


def gram_kernel(nr, nc, part_ref, out_ref, heard, total, blocks, send, recv, give, take, pass_on, get):
    my_row = lax.axis_index("row")
    my_col = lax.axis_index("col")
    size = part_ref.shape[0] // nr
    wide = part_ref.shape[1]
    mesh_id = pl.DeviceIdType.MESH

    def rows_of(row):
        return pl.ds(pl.multiple_of(row * size, size), size)

    def row_peer(k):
        return lax.rem(my_row + k, nr)

    def col_peer(j):
        return lax.rem(my_col + j, nc)

    barrier = pltpu.get_barrier_semaphore()
    for k in range(1, nr):
        pl.semaphore_signal(barrier, inc=1, device_id=(row_peer(k), my_col), device_id_type=mesh_id)
    for j in range(1, nc):
        pl.semaphore_signal(barrier, inc=1, device_id=(my_row, col_peer(j)), device_id_type=mesh_id)
    pl.semaphore_wait(barrier, nr + nc - 2)

    first = [
        pltpu.make_async_remote_copy(
            src_ref=part_ref.at[rows_of(row_peer(k))],
            dst_ref=heard.at[k],
            send_sem=send.at[k],
            recv_sem=recv.at[k],
            device_id=(row_peer(k), my_col),
            device_id_type=mesh_id,
        )
        for k in range(1, nr)
    ]
    for copy in first:
        copy.start()
    value = part_ref[rows_of(my_row), :]
    for k, copy in enumerate(first, 1):
        copy.wait_recv()
        value = value + heard[k]
    total[...] = value

    def spread(k, j, block):
        return pltpu.make_async_remote_copy(
            src_ref=block,
            dst_ref=blocks.at[my_col, rows_of(lax.rem(my_row - k + nr, nr))],
            send_sem=pass_on.at[k, j],
            recv_sem=get.at[k, j],
            device_id=(my_row, col_peer(j)),
            device_id_type=mesh_id,
        )

    second = [
        pltpu.make_async_remote_copy(
            src_ref=total,
            dst_ref=blocks.at[my_col, rows_of(my_row)],
            send_sem=give.at[k],
            recv_sem=take.at[k],
            device_id=(row_peer(k), my_col),
            device_id_type=mesh_id,
        )
        for k in range(1, nr)
    ]
    for copy in second:
        copy.start()
    third = [spread(0, j, total) for j in range(1, nc)]
    for copy in third:
        copy.start()
    blocks[my_col, rows_of(my_row), :] = value
    for k, copy in enumerate(second, 1):
        copy.wait_recv()
        block = blocks.at[my_col, rows_of(lax.rem(my_row - k + nr, nr))]
        for j in range(1, nc):
            hop = spread(k, j, block)
            hop.start()
            third.append(hop)
    for copy in third:
        copy.wait_recv()
    for c in range(nc):
        out_ref[:, c * wide : (c + 1) * wide] = blocks[c]
    for copy in first + second + third:
        copy.wait_send()


def sum_gram(part, nr, nc):
    width, wide = part.shape
    spec = pl.BlockSpec(memory_space=pltpu.VMEM)
    dma = pltpu.SemaphoreType.DMA
    return pl.pallas_call(
        functools.partial(gram_kernel, nr, nc),
        out_shape=jax.ShapeDtypeStruct((width, wide * nc), jnp.float32),
        in_specs=[spec],
        out_specs=spec,
        scratch_shapes=[
            pltpu.VMEM((nr, width // nr, wide), jnp.float32),
            pltpu.VMEM((width // nr, wide), jnp.float32),
            pltpu.VMEM((nc, width, wide), jnp.float32),
            dma((nr,)),
            dma((nr,)),
            dma((nr,)),
            dma((nr,)),
            dma((nr, nc)),
            dma((nr, nc)),
        ],
        compiler_params=pltpu.CompilerParams(collective_id=0, has_side_effects=True),
        cost_estimate=pl.CostEstimate(
            flops=100000, bytes_accessed=20000000, transcendentals=0
        ),
        name="sum_gram",
    )(part)


def split2(x):
    top = x.astype(jnp.bfloat16)
    return top, (x - top.astype(jnp.float32)).astype(jnp.bfloat16)


def update_kernel(panel_ref, weights_ref, trailing_ref, out_ref, top, low):
    @pl.when(pl.program_id(0) == 0)
    def _():
        top[...], low[...] = split2(weights_ref[...])

    pt, pm = split2(panel_ref[...])

    def product(left, right):
        return jnp.dot(left, right[...], preferred_element_type=jnp.float32)

    out_ref[...] = trailing_ref[...] - (product(pt, top) + (product(pt, low) + product(pm, top)))


def update(panel, weights, trailing):
    rows, width = panel.shape
    columns = trailing.shape[1]
    tile = next((t for t in (384, 256, 128, 64, 8) if rows % t == 0), rows)
    return pl.pallas_call(
        update_kernel,
        grid=(rows // tile,),
        out_shape=jax.ShapeDtypeStruct(trailing.shape, jnp.float32),
        in_specs=[
            pl.BlockSpec((tile, width), lambda i: (i, 0)),
            pl.BlockSpec((width, columns), lambda i: (0, 0)),
            pl.BlockSpec((tile, columns), lambda i: (i, 0)),
        ],
        out_specs=pl.BlockSpec((tile, columns), lambda i: (i, 0)),
        scratch_shapes=[pltpu.VMEM((width, columns), jnp.bfloat16)] * 2,
        cost_estimate=pl.CostEstimate(
            flops=6 * rows * width * columns,
            bytes_accessed=4 * (rows * width + 2 * rows * columns),
            transcendentals=0,
        ),
        name="update",
    )(panel, weights, trailing)


def on_device(nr, nc, panel_block, trailing):
    gathered = lax.all_gather(panel_block, "col", axis=1, tiled=True)
    share = inner_products(gathered, trailing)
    projected = lax.psum(share, "row")
    gathered, share = lax.optimization_barrier((gathered, share))
    gram = sum_gram(inner_products(gathered, panel_block), nr, nc)
    upper, inverse = factor(gram)
    coupling = matmul(inverse, projected)
    weights = inner_products(inverse, coupling)
    updated = update(gathered, weights, trailing)
    return (upper, coupling, updated)


def solution(mesh):
    placed = (P("row", "col"), P("row", "col"))
    return jax.shard_map(
        functools.partial(on_device, mesh.shape["row"], mesh.shape["col"]),
        mesh=mesh,
        in_specs=placed,
        out_specs=(P(), P(None, "col"), P("row", "col")),
        check_vma=False,
    )
```

```python
import functools

import jax
import jax.numpy as jnp
from jax import lax
from jax.experimental import pallas as pl
from jax.experimental.pallas import tpu as pltpu
from jax.sharding import PartitionSpec as P

LANES = 128
SUB = 8
highest = lax.Precision.HIGHEST
high = lax.Precision.HIGH


def inner_products(left, right, precision=high):
    return lax.dot_general(
        left, right, (((0,), (0,)), ((), ())), precision=precision, preferred_element_type=jnp.float32
    )


def matmul(left, right, precision=high):
    return jnp.dot(left, right, precision=precision, preferred_element_type=jnp.float32)


def split3(x):
    top = x.astype(jnp.bfloat16).astype(jnp.float32)
    rest = x - top
    mid = rest.astype(jnp.bfloat16).astype(jnp.float32)
    return top, mid, rest - mid


def rank_update(left, right):
    lt, lm, ll = split3(left)
    rt, rm, rl = split3(right)
    a = jnp.concatenate([lt, lt, lm, lt, ll, lm], axis=0).astype(jnp.bfloat16)
    b = jnp.concatenate([rt, rm, rt, rl, rt, rm], axis=0).astype(jnp.bfloat16)
    return lax.dot_general(a, b, (((0,), (0,)), ((), ())), preferred_element_type=jnp.float32)


def factor_diagonal(square):
    lane = lax.broadcasted_iota(jnp.int32, (SUB, LANES), 1)
    sub = lax.broadcasted_iota(jnp.int32, (SUB, LANES), 0)
    full = (SUB, LANES)
    work = square
    upper_rows, inverse_rows = [], []
    for first in range(0, LANES, SUB):
        rows = work[:SUB]
        b = [jnp.broadcast_to(rows[t : t + 1, :], full) for t in range(SUB)]
        d = [
            [None if s < t else jnp.broadcast_to(b[t][:, first + s : first + s + 1], full) for s in range(SUB)]
            for t in range(SUB)
        ]
        inside = (lane >= first) & (lane < first + SUB)
        unit = [jnp.where(inside, jnp.where(lane == first + t, 1.0, 0.0), b[t]) for t in range(SUB)]
        tri = jnp.zeros(full, jnp.float32)
        out = jnp.zeros(full, jnp.float32)
        for t in range(SUB):
            inv = 1.0 / jnp.sqrt(d[t][t])
            for s in range(t, SUB):
                d[t][s] = d[t][s] * inv
            x = unit[t] * inv
            for s in range(t + 1, SUB):
                for q in range(s, SUB):
                    d[s][q] = d[s][q] - d[t][s] * d[t][q]
                unit[s] = unit[s] - d[t][s] * x
            line = x
            for s in range(SUB):
                line = jnp.where(lane == first + s, d[t][s] if s >= t else 0.0, line)
            tri = jnp.where(sub == t, line, tri)
            out = jnp.where(sub == t, x, out)
        upper_rows.append(jnp.where(lane >= first, tri, 0.0))
        inverse_rows.append(jnp.where(lane < first + SUB, out, 0.0))
        if first + SUB < LANES:
            beyond = jnp.where(lane >= first + SUB, out, 0.0)
            left = work[SUB:]
            place = lax.broadcasted_iota(jnp.int32, left.shape, 1)
            left = jnp.where((place >= first) & (place < first + SUB), 0.0, left)
            work = left - rank_update(beyond, out)[first + SUB :]
    return jnp.concatenate(upper_rows, axis=0), jnp.concatenate(inverse_rows, axis=0)


def factor_kernel(gram_ref, upper_ref, inverse_ref, work):
    width = gram_ref.shape[0]
    work[...] = gram_ref[...]
    upper_ref[...] = jnp.zeros_like(upper_ref)
    inverse_ref[...] = jnp.zeros_like(inverse_ref)
    lanes_all = lax.broadcasted_iota(jnp.int32, (LANES, width), 1)

    @pl.loop(0, width // LANES)
    def _(k):
        at = pl.multiple_of(k * LANES, LANES)
        here = pl.ds(at, LANES)
        upper, inverse = factor_diagonal(work[here, here])
        rows = matmul(inverse, work[here, :], highest)
        upper_ref[here, :] = jnp.where(lanes_all >= at + LANES, rows, 0.0)
        upper_ref[here, here] = upper
        inverse_ref[here, :] = jnp.where(lanes_all < at, rows, 0.0)
        inverse_ref[here, here] = inverse
        work[here, :] = rows
        work[here, here] = inverse
        done = work[here, :]
        right = upper_ref[here, :]
        for i in range(1, width // LANES):
            @pl.when(i > k)
            def _():
                block = slice(i * LANES, (i + 1) * LANES)
                below = inner_products(right[:, block], done, highest)
                old = jnp.where((lanes_all >= at) & (lanes_all < at + LANES), 0.0, work[block, :])
                work[block, :] = old - below


def factor(gram):
    width = gram.shape[0]
    spec = pl.BlockSpec(memory_space=pltpu.VMEM)
    shape = jax.ShapeDtypeStruct((width, width), jnp.float32)
    return pl.pallas_call(
        factor_kernel,
        out_shape=(shape, shape),
        in_specs=[spec],
        out_specs=(spec, spec),
        scratch_shapes=[pltpu.VMEM((width, width), jnp.float32)],
        cost_estimate=pl.CostEstimate(
            flops=4 * width**3, bytes_accessed=12 * width * width, transcendentals=100000
        ),
        name="factor",
    )(gram)


def gram_kernel(nr, nc, part_ref, out_ref, heard, total, blocks, send, recv, give, take, pass_on, get):
    my_row = lax.axis_index("row")
    my_col = lax.axis_index("col")
    size = part_ref.shape[0] // nr
    wide = part_ref.shape[1]
    mesh_id = pl.DeviceIdType.MESH

    def rows_of(row):
        return pl.ds(pl.multiple_of(row * size, size), size)

    def row_peer(k):
        return lax.rem(my_row + k, nr)

    def col_peer(j):
        return lax.rem(my_col + j, nc)

    barrier = pltpu.get_barrier_semaphore()
    for k in range(1, nr):
        pl.semaphore_signal(barrier, inc=1, device_id=(row_peer(k), my_col), device_id_type=mesh_id)
    for j in range(1, nc):
        pl.semaphore_signal(barrier, inc=1, device_id=(my_row, col_peer(j)), device_id_type=mesh_id)
    pl.semaphore_wait(barrier, nr + nc - 2)

    first = [
        pltpu.make_async_remote_copy(
            src_ref=part_ref.at[rows_of(row_peer(k))],
            dst_ref=heard.at[k],
            send_sem=send.at[k],
            recv_sem=recv.at[k],
            device_id=(row_peer(k), my_col),
            device_id_type=mesh_id,
        )
        for k in range(1, nr)
    ]
    for copy in first:
        copy.start()
    value = part_ref[rows_of(my_row), :]
    for k, copy in enumerate(first, 1):
        copy.wait_recv()
        value = value + heard[k]
    total[...] = value

    def spread(k, j, block):
        return pltpu.make_async_remote_copy(
            src_ref=block,
            dst_ref=blocks.at[my_col, rows_of(lax.rem(my_row - k + nr, nr))],
            send_sem=pass_on.at[k, j],
            recv_sem=get.at[k, j],
            device_id=(my_row, col_peer(j)),
            device_id_type=mesh_id,
        )

    second = [
        pltpu.make_async_remote_copy(
            src_ref=total,
            dst_ref=blocks.at[my_col, rows_of(my_row)],
            send_sem=give.at[k],
            recv_sem=take.at[k],
            device_id=(row_peer(k), my_col),
            device_id_type=mesh_id,
        )
        for k in range(1, nr)
    ]
    for copy in second:
        copy.start()
    third = [spread(0, j, total) for j in range(1, nc)]
    for copy in third:
        copy.start()
    blocks[my_col, rows_of(my_row), :] = value
    for k, copy in enumerate(second, 1):
        copy.wait_recv()
        block = blocks.at[my_col, rows_of(lax.rem(my_row - k + nr, nr))]
        for j in range(1, nc):
            hop = spread(k, j, block)
            hop.start()
            third.append(hop)
    for copy in third:
        copy.wait_recv()
    for c in range(nc):
        out_ref[:, c * wide : (c + 1) * wide] = blocks[c]
    for copy in first + second + third:
        copy.wait_send()


def sum_gram(part, nr, nc):
    width, wide = part.shape
    spec = pl.BlockSpec(memory_space=pltpu.VMEM)
    dma = pltpu.SemaphoreType.DMA
    return pl.pallas_call(
        functools.partial(gram_kernel, nr, nc),
        out_shape=jax.ShapeDtypeStruct((width, wide * nc), jnp.float32),
        in_specs=[spec],
        out_specs=spec,
        scratch_shapes=[
            pltpu.VMEM((nr, width // nr, wide), jnp.float32),
            pltpu.VMEM((width // nr, wide), jnp.float32),
            pltpu.VMEM((nc, width, wide), jnp.float32),
            dma((nr,)),
            dma((nr,)),
            dma((nr,)),
            dma((nr,)),
            dma((nr, nc)),
            dma((nr, nc)),
        ],
        compiler_params=pltpu.CompilerParams(collective_id=0, has_side_effects=True),
        cost_estimate=pl.CostEstimate(
            flops=100000, bytes_accessed=20000000, transcendentals=0
        ),
        name="sum_gram",
    )(part)


def split2(x):
    top = x.astype(jnp.bfloat16)
    return top, (x - top.astype(jnp.float32)).astype(jnp.bfloat16)


def update_kernel(panel_ref, weights_ref, trailing_ref, out_ref, top, low):
    @pl.when(pl.program_id(0) == 0)
    def _():
        top[...], low[...] = split2(weights_ref[...])

    pt, pm = split2(panel_ref[...])

    def product(left, right):
        return jnp.dot(left, right[...], preferred_element_type=jnp.float32)

    out_ref[...] = trailing_ref[...] - (product(pt, top) + (product(pt, low) + product(pm, top)))


def update(panel, weights, trailing):
    rows, width = panel.shape
    columns = trailing.shape[1]
    tile = next((t for t in (384, 256, 128, 64, 8) if rows % t == 0), rows)
    return pl.pallas_call(
        update_kernel,
        grid=(rows // tile,),
        out_shape=jax.ShapeDtypeStruct(trailing.shape, jnp.float32),
        in_specs=[
            pl.BlockSpec((tile, width), lambda i: (i, 0)),
            pl.BlockSpec((width, columns), lambda i: (0, 0)),
            pl.BlockSpec((tile, columns), lambda i: (i, 0)),
        ],
        out_specs=pl.BlockSpec((tile, columns), lambda i: (i, 0)),
        scratch_shapes=[pltpu.VMEM((width, columns), jnp.bfloat16)] * 2,
        cost_estimate=pl.CostEstimate(
            flops=6 * rows * width * columns,
            bytes_accessed=4 * (rows * width + 2 * rows * columns),
            transcendentals=0,
        ),
        name="update",
    )(panel, weights, trailing)


def gather_kernel(nc, pieces, block_ref, out_ref, send, recv, pass_on, get, near):
    my_row = lax.axis_index("row")
    my_col = lax.axis_index("col")
    rows, wide = block_ref.shape
    size = rows // pieces
    mesh_id = pl.DeviceIdType.MESH
    core = lax.rem(my_col, 2)
    partner = my_col + 1 - 2 * core

    def across(j):
        return lax.rem(my_col + 2 * j, nc)

    def columns(col):
        return pl.ds(pl.multiple_of(col * wide, wide), wide)

    def remote(src, dst, send_sem, recv_sem, col):
        return pltpu.make_async_remote_copy(
            src_ref=src, dst_ref=dst, send_sem=send_sem, recv_sem=recv_sem,
            device_id=(my_row, col), device_id_type=mesh_id,
        )

    barrier = pltpu.get_barrier_semaphore()
    pl.semaphore_signal(barrier, inc=1, device_id=(my_row, partner), device_id_type=mesh_id)
    for j in range(1, nc // 2):
        pl.semaphore_signal(barrier, inc=1, device_id=(my_row, across(j)), device_id_type=mesh_id)
    pl.semaphore_wait(barrier, nc // 2)

    far = []
    for p in range(pieces):
        here = pl.ds(p * size, size)
        for j in range(1, nc // 2):
            copy = remote(
                block_ref.at[here], out_ref.at[here, columns(my_col)],
                send.at[j, p], recv.at[j, p], across(j),
            )
            copy.start()
            far.append((p, j, copy))
    beside = remote(block_ref, out_ref.at[:, columns(my_col)], near.at[0], near.at[1], partner)
    beside.start()
    own = pltpu.make_async_copy(block_ref, out_ref.at[:, columns(my_col)], near.at[2])
    own.start()
    hops = []
    for p, j, copy in far:
        copy.wait_recv()
        source = lax.rem(my_col - 2 * j + nc, nc)
        spot = out_ref.at[pl.ds(p * size, size), columns(source)]
        hop = remote(spot, spot, pass_on.at[j, p], get.at[j, p], partner)
        hop.start()
        hops.append(hop)
    own.wait()
    beside.wait()
    for hop in hops:
        hop.wait()
    for _, _, copy in far:
        copy.wait_send()


def gather_panel(block, nc):
    rows, wide = block.shape
    pieces = 8
    if nc % 2 or wide % LANES or rows % (SUB * pieces):
        return lax.all_gather(block, "col", axis=1, tiled=True)
    dma = pltpu.SemaphoreType.DMA
    return pl.pallas_call(
        functools.partial(gather_kernel, nc, pieces),
        out_shape=jax.ShapeDtypeStruct((rows, wide * nc), jnp.float32),
        in_specs=[pl.BlockSpec(memory_space=pltpu.VMEM)],
        out_specs=pl.BlockSpec(memory_space=pl.ANY),
        scratch_shapes=[dma((nc // 2, pieces))] * 4 + [dma((3,))],
        compiler_params=pltpu.CompilerParams(collective_id=1, has_side_effects=True),
        name="gather_panel",
    )(block)


def on_device(nr, nc, panel_block, trailing):
    gathered = gather_panel(panel_block, nc)
    share = inner_products(gathered, trailing)
    projected = lax.psum(share, "row")
    gathered, share = lax.optimization_barrier((gathered, share))
    gram = sum_gram(inner_products(gathered, panel_block), nr, nc)
    upper, inverse = factor(gram)
    coupling = matmul(inverse, projected)
    weights = inner_products(inverse, coupling)
    updated = update(gathered, weights, trailing)
    return (upper, coupling, updated)


def solution(mesh):
    placed = (P("row", "col"), P("row", "col"))
    return jax.shard_map(
        functools.partial(on_device, mesh.shape["row"], mesh.shape["col"]),
        mesh=mesh,
        in_specs=placed,
        out_specs=(P(), P(None, "col"), P("row", "col")),
        check_vma=False,
    )
```
